32 devices in a mesh: parts: 2 (over x), pts: 16 (over z, y, core).
Axes of the slice: x: 2, y: 2, z: 4, core: 2. Of those that a mesh axis runs over, the one named last changes fastest.
Arguments:
- grid_weights: float32 [256, 128, 128], P(('parts', 'pts')), parts along dimension 0, may hold values from -6 to 6
- direction: float32 [256, 128, 128], P(('parts', 'pts')), parts along dimension 0, may hold values from -6 to 6
- kern_x: float32 [128, 128], replicated
- kern_y: float32 [128, 128], replicated
- kern_z: float32 [128, 128], replicated
- interp: bfloat16 [4096, 128, 256], P(('parts', 'pts')), parts along dimension 0, may hold values from -4 to 4
- block_corner: int32 [3, 4096], P(None, ('parts', 'pts')), parts along dimension 1, may hold values from 0 to 120, as said below
- block_offsets: int32 [4096, 256], P(('parts', 'pts')), parts along dimension 0, may hold values from 0 to 2047, as said below
- labels: int32 [4096, 128], P(('parts', 'pts')), parts along dimension 0, may hold values 0 or 1
- trial_steps: float32 [5], replicated, may hold values from 0.05 to 2
- accept: int32 [1], replicated, may hold values from 0 to 4
Outputs:
- new_weights: float32 [256, 128, 128], P(('parts', 'pts')), parts along dimension 0
- grid_gradient: float32 [256, 128, 128], P(('parts', 'pts')), parts along dimension 0
- curvature: float32 [4096, 128], P(('parts', 'pts')), parts along dimension 0
- trial_objective: float32 [10], P('parts'), parts along dimension 0
- trial_slope: float32 [10], P('parts'), parts along dimension 0
The draws below stay inside these ranges and needn't reach their ends.
There are 2 independent parts, one for each index of `parts`. The reference program is written for one: setup_inputs(seed, part) draws one part's arguments, and reference() takes and returns one part's arrays. A program takes and returns all parts, laid end to end along the dimension named above; an argument that names none is the same for every part. Nothing has to cross between parts.
Inputs may be any that keep to these rules, and one draw needn't show every extreme that they name: `block_corner`: row 0 lies in 0 to 112, row 1 in 0 to 112, row 2 in 0 to 120. `block_offsets`: the 256 offsets of one block are distinct.
All inputs are finite; a program needn't handle non-finite values. No bound on the sum of `labels` on one device may be relied on, other than what follows from the above.
Results may differ from the reference program's by a relative error of at most 0.0075.
The reference program's roundings to bfloat16 on the way count: a program that leaves them out, or rounds other values in their place, can miss the bound.
Values may be sent and summed in bfloat16 or wider, within the bound.
A program may use at most 128 MiB of HBM per device.

```python
import math
import jax
import jax.numpy as jnp
from jax import lax

GX = 128
GY = 128
GZ = 128
BOXX = 16
BOXY = 16
BOXZ = 8
COLS = 256
PTS_BLOCK = 128
NTRIAL = 5
NB = 128
BLOCKS = 2048
POINTS = 262144
N_PTS = 16


def kernel_table(key, size, salt):
    key = jax.random.fold_in(key, salt)
    key_len, key_noise, key_gain = jax.random.split(key, 3)
    length = jax.random.uniform(key_len, (), jnp.float32, 4.0, 16.0)
    noise_scale = 0.15
    position = jnp.arange(size, dtype=jnp.float32)
    spacing = jnp.abs(position[:, None] - position[None, :])
    smooth = jnp.exp(-spacing / length)
    noise = jax.random.normal(key_noise, (size, size), jnp.float32)
    symmetric = (noise + noise.T) * 0.7071
    gains = jax.random.uniform(key_gain, (size,), jnp.float32, 0.7, 1.4)
    table = gains[:, None] * (smooth + noise_scale * symmetric) * gains[None, :] / jnp.sqrt(length)
    return table.astype(jnp.float32)


def draw_kern_x(key, part):
    return kernel_table(key, GX, 11)


def draw_kern_y(key, part):
    return kernel_table(key, GY, 23)


def draw_kern_z(key, part):
    return kernel_table(key, GZ, 37)


def draw_interp(key, part):
    key = jax.random.fold_in(key, 53)
    ratio = 6.0
    base = jnp.clip(jax.random.normal(key, (BLOCKS, PTS_BLOCK, COLS), jnp.float32), -4.0, 4.0)
    level = jnp.arange(BLOCKS, dtype=jnp.float32) / max(BLOCKS - 1, 1)
    scale = jnp.exp(jnp.log(ratio) * level) / jnp.sqrt(ratio)
    table = base * scale[:, None, None] / jnp.sqrt(jnp.float32(COLS))
    return jnp.clip(table, -4.0, 4.0).astype(jnp.bfloat16)


def draw_block_corner(key, part):
    limits = jnp.array([GX - BOXX, GY - BOXY, GZ - BOXZ], jnp.int32)
    corner = jax.random.randint(key, (3, BLOCKS), 0, limits[:, None] + 1)
    corner = corner.at[:, 0].set(limits)
    corner = corner.at[:, BLOCKS - 1].set(0)
    return corner.astype(jnp.int32)


def draw_block_offsets(key, part):
    keys = jax.random.split(key, BLOCKS)

    def choose_cells(one_key):
        return jax.random.permutation(one_key, BOXX * BOXY * BOXZ)[:COLS]
    return jax.vmap(choose_cells)(keys).astype(jnp.int32)


def place_ends(values, rng, smallest, top_value):
    longest = values.shape.index(max(values.shape))
    spots = []
    for shift in (0, 1):
        where = [jax.random.randint(jax.random.fold_in(rng, axis), (), 0, length) for axis, length in enumerate(values.shape)]
        where[longest] = (where[longest] + shift) % values.shape[longest]
        spots.append(tuple(where))
    return values.at[spots[0]].set(smallest).at[spots[1]].set(top_value)


def levels(rng, shape, pieces, smallest, top_value):
    def one(dim, blocks):
        steps = jax.random.uniform(jax.random.fold_in(jax.random.fold_in(rng, 6), dim), (blocks,), jnp.float32, smallest / len(pieces), top_value / len(pieces))
        return jnp.repeat(jnp.exp(steps), shape[dim] // blocks).reshape((-1,) + (1,) * (len(shape) - dim - 1))

    level = one(*pieces[0])
    for cut in pieces[1:]:
        level = level * one(*cut)
    return level


def bell_draw(rng, dims, width, limit, shards=(), held_as=jnp.bfloat16):
    values = width * jax.random.normal(rng, dims, jnp.float32)
    if shards:
        values = values * levels(rng, dims, shards, -0.22, 0.18)
    return jnp.clip(values, -limit, limit).astype(held_as)


def setup_inputs(seed: int = 0, part: int = 0) -> dict:
    key_list = jax.random.split(jax.random.key(seed), 12)
    own_keys = jax.random.split(jax.random.fold_in(key_list[11], part), 12)
    grid_weights = bell_draw(own_keys[0], (GX, GY, GZ), 1.0, 6.0, ((0, 16),), jnp.float32)
    direction = bell_draw(own_keys[1], (GX, GY, GZ), 1.0, 6.0, ((0, 16),), jnp.float32)
    kern_x = draw_kern_x(jax.random.fold_in(key_list[11], 71), part)
    kern_y = draw_kern_y(jax.random.fold_in(key_list[11], 71), part)
    kern_z = draw_kern_z(jax.random.fold_in(key_list[11], 71), part)
    interp = draw_interp(jax.random.fold_in(jax.random.fold_in(key_list[11], part), 71), part)
    block_corner = draw_block_corner(jax.random.fold_in(jax.random.fold_in(key_list[11], part), 71), part)
    block_offsets = draw_block_offsets(jax.random.fold_in(jax.random.fold_in(key_list[11], part), 71), part)
    labels = place_ends((jax.random.randint(own_keys[8], (BLOCKS, PTS_BLOCK), 0, 2) < 1).astype(jnp.int32), jax.random.fold_in(own_keys[8], 1), 0, 1)
    trial_steps = jnp.clip(jnp.exp(jax.random.uniform(key_list[9], (NTRIAL,), jnp.float32, math.log(0.05), math.log(2.0))), 0.05, 2.0)
    accept = jax.random.randint(key_list[10], (1,), 0, NTRIAL).astype(jnp.int32)
    return dict(grid_weights=grid_weights, direction=direction, kern_x=kern_x, kern_y=kern_y, kern_z=kern_z, interp=interp, block_corner=block_corner, block_offsets=block_offsets, labels=labels, trial_steps=trial_steps, accept=accept)


HIGHEST = lax.Precision.HIGHEST


def plane_mix(fields, kern_y, kern_z):
    inner_mix = jnp.einsum('...bc,zc->...bz', fields, kern_z, precision=HIGHEST)
    return jnp.einsum('...xbz,yb->...xyz', inner_mix, kern_y, precision=HIGHEST).astype(jnp.bfloat16)


def depth_mix(partial_value, kern_x):
    return jnp.einsum('xa,...ayz->...xyz', kern_x, partial_value.astype(jnp.float32), precision=HIGHEST)


def cell_ids_of(block_corner, block_offsets):
    plane_off = block_offsets // (BOXY * BOXZ)
    row_off = (block_offsets // BOXZ) % BOXY
    depth_off = block_offsets % BOXZ
    cell_x = block_corner[0][:, None] + plane_off
    cell_y = block_corner[1][:, None] + row_off
    cell_z = block_corner[2][:, None] + depth_off
    return ((cell_x * GY + cell_y) * GZ + cell_z).astype(jnp.int32)


def interpolate(interp, values):
    count_fields = values.shape[0]
    groups = interp.reshape(N_PTS, NB, PTS_BLOCK, COLS)
    grouped = jnp.moveaxis(values.reshape(count_fields, N_PTS, NB, COLS), 1, 0)

    def one_group(operands):
        return jnp.einsum('bpc,fbc->fbp', operands[0].astype(jnp.float32), operands[1].astype(jnp.float32), precision=HIGHEST)

    result = lax.map(one_group, (groups, grouped))
    return jnp.moveaxis(result, 0, 1).reshape(count_fields, N_PTS * NB, PTS_BLOCK)


def column_terms(interp, residual):
    groups = interp.reshape(N_PTS, NB, PTS_BLOCK, COLS)
    grouped = residual.reshape(N_PTS, NB, PTS_BLOCK)

    def one_group(operands):
        return jnp.einsum('bpc,bp->bc', operands[0].astype(jnp.float32), operands[1].astype(jnp.float32), precision=HIGHEST)

    return lax.map(one_group, (groups, grouped)).reshape(N_PTS * NB, COLS)


def reference(grid_weights, direction, kern_x, kern_y, kern_z, interp, block_corner, block_offsets, labels, trial_steps, accept):
    fields = jnp.stack([grid_weights, direction])
    mixed_grid = depth_mix(plane_mix(fields, kern_y, kern_z), kern_x)
    quad_gu = jnp.sum(grid_weights * mixed_grid[0])
    quad_du = jnp.sum(direction * mixed_grid[0])
    quad_dv = jnp.sum(direction * mixed_grid[1])
    cell_ids = cell_ids_of(block_corner, block_offsets)
    flat_grid = mixed_grid.astype(jnp.bfloat16).reshape(2, -1)
    values = jnp.take(flat_grid, cell_ids, axis=1)
    latent_pair = interpolate(interp, values)
    latent = latent_pair[0]
    slope_pt = latent_pair[1]
    target = labels.astype(jnp.float32)
    signed = 2.0 * target - 1.0
    trial_latent = latent[None] + trial_steps[:, None, None] * slope_pt[None]
    loglik = jnp.sum(jax.nn.log_sigmoid(signed[None] * trial_latent), axis=(1, 2))
    descent = jnp.sum((target[None] - jax.nn.sigmoid(trial_latent)) * slope_pt[None], axis=(1, 2))
    prior = 0.5 * (quad_gu + 2.0 * trial_steps * quad_du + trial_steps * trial_steps * quad_dv)
    trial_objective = (loglik - prior) / POINTS
    trial_slope = (descent - quad_du - trial_steps * quad_dv) / POINTS
    chosen = jnp.sum(jnp.where(jnp.arange(NTRIAL) == accept[0], trial_steps, 0.0))
    probability = jax.nn.sigmoid(latent + chosen * slope_pt)
    residual = (target - probability).astype(jnp.bfloat16)
    column_term = column_terms(interp, residual)
    spread = jnp.zeros((GX * GY * GZ,), jnp.float32).at[cell_ids.reshape(-1)].add(column_term.reshape(-1)).reshape(GX, GY, GZ)
    new_weights = grid_weights + chosen * direction
    grid_gradient = spread - new_weights
    bend_grid = depth_mix(plane_mix(grid_gradient[None], kern_y, kern_z), kern_x)
    bend_values = jnp.take(bend_grid.astype(jnp.bfloat16).reshape(1, -1), cell_ids, axis=1)
    bend_pt = interpolate(interp, bend_values)[0]
    curvature = probability * (1.0 - probability) * bend_pt
    return new_weights, grid_gradient, curvature, trial_objective, trial_slope
```

```python
import functools

import jax
import jax.numpy as jnp
from jax import lax
from jax.experimental import pallas as pl
from jax.experimental.pallas import tpu as pltpu
from jax.sharding import PartitionSpec as P

BOXX = 16
BOXY = 16
BOXZ = 8
NTRIAL = 5
PACK = 16
VMEM_BYTES = 60 * 1024 * 1024

HIGHEST = lax.Precision.HIGHEST
F32 = jnp.float32
BF16 = jnp.bfloat16
NT = (((1,), (1,)), ((), ()))


def high_part(value):
    return lax.reduce_precision(value, 8, 7)


def plane_mix(fields_zc, kern_y, kern_z):
    inner = jnp.einsum("zc,fabc->zfab", kern_z, fields_zc, precision=HIGHEST)
    return jnp.einsum("zfab,yb->zfay", inner, kern_y, precision=HIGHEST).astype(BF16)


def widen_kern(kern_x, devices, slab, group):
    size_x = kern_x.shape[0]
    parts = kern_x.reshape(1, size_x, devices, 1, slab)
    same = jnp.eye(group, dtype=F32).reshape(group, 1, 1, group, 1)
    wide = (parts * same).reshape(group * size_x, devices * group * slab)
    high = high_part(wide)
    return high.astype(BF16), (wide - high).astype(BF16)


def mix_depth(planes_ref, kh_ref, kl_ref, image, group, size_x):
    devices, units, pack, lanes = planes_ref.shape

    def one(step, carry):
        pair = [
            planes_ref[:, step * 2 + t].reshape(devices * pack, lanes) for t in range(2)
        ]
        rhs = jnp.concatenate(pair, axis=1)
        mixed = jnp.dot(kh_ref[...], rhs, preferred_element_type=F32)
        mixed = mixed + jnp.dot(kl_ref[...], rhs, preferred_element_type=F32)
        for t in range(2):
            for g in range(group):
                image[(step * 2 + t) * group + g] = mixed[
                    g * size_x : (g + 1) * size_x, t * lanes : (t + 1) * lanes
                ]
        return carry

    lax.fori_loop(0, units // 2, one, 0)


def pick_values(image, corner_ref, y_ref, row_ref, block, local, fields):
    size_y = image.shape[-1]
    cols = y_ref.shape[-1]
    box_rows = BOXZ * BOXX
    at_z = corner_ref[2, block]
    at_x = corner_ref[0, block]
    box = image[pl.ds(at_z * fields, BOXZ * fields), pl.ds(at_x, BOXX), :]
    box = box.reshape(fields * box_rows, size_y).astype(BF16)
    y_line = lax.broadcasted_iota(jnp.int32, (size_y, cols), 0)
    pick_y = jnp.where(y_line == y_ref[pl.ds(local, 1), :], 1.0, 0.0).astype(BF16)
    lines = jnp.dot(box, pick_y, preferred_element_type=F32)
    lines = lines.reshape(BOXZ, fields, BOXX, cols)
    row_line = lax.broadcasted_iota(jnp.int32, (box_rows, cols), 0)
    kept = row_line == row_ref[pl.ds(local, 1), :]
    top = lax.broadcasted_iota(jnp.int32, (8, cols), 0)
    stacked = jnp.zeros((8, cols), F32)
    for f in range(fields):
        line = jnp.where(kept, lines[:, f].reshape(box_rows, cols), 0.0)
        value = jnp.sum(line, axis=0, keepdims=True)
        stacked = jnp.where(top == f, value, stacked)
    return stacked.astype(BF16)


def forward_kernel(
    group,
    unroll,
    corner_ref,
    slab_ref,
    chosen_ref,
    planes_ref,
    kh_ref,
    kl_ref,
    y_ref,
    row_ref,
    labels_ref,
    interp_ref,
    latent_ref,
    prob_ref,
    col_ref,
    own_ref,
    image,
    res_ref,
):
    step = pl.program_id(0)
    count = interp_ref.shape[0]
    size_x = image.shape[1]

    @pl.when(step == 0)
    def _():
        mix_depth(planes_ref, kh_ref, kl_ref, image, group, size_x)
        slab = own_ref.shape[1]
        at = pl.multiple_of(slab_ref[0] * slab, slab)
        own_ref[...] = image[:, pl.ds(at, slab), :]

    def some(part, carry):
        for k in range(unroll):
            local = part * unroll + k
            values = pick_values(
                image, corner_ref, y_ref, row_ref, step * count + local, local, 2
            )
            pair = lax.dot_general(values, interp_ref[local], NT, preferred_element_type=F32)
            latent_ref[0, pl.ds(local, 1), :] = pair[0:1]
            latent_ref[1, pl.ds(local, 1), :] = pair[1:2]
        return carry

    lax.fori_loop(0, count // unroll, some, 0)
    logits = latent_ref[0] + chosen_ref[0] * latent_ref[1]
    prob = jax.nn.sigmoid(logits)
    prob_ref[...] = prob
    res_ref[...] = (labels_ref[...].astype(F32) - prob).astype(BF16).astype(F32)

    def back(part, carry):
        for k in range(unroll):
            local = part * unroll + k
            row = jnp.broadcast_to(res_ref[pl.ds(local, 1), :], (8, res_ref.shape[1]))
            term = jnp.dot(row.astype(BF16), interp_ref[local], preferred_element_type=F32)
            col_ref[pl.ds(local, 1), :] = term[0:1]
        return carry

    lax.fori_loop(0, count // unroll, back, 0)


def bend_kernel(
    group,
    unroll,
    corner_ref,
    planes_ref,
    kh_ref,
    kl_ref,
    y_ref,
    row_ref,
    prob_ref,
    interp_ref,
    out_ref,
    image,
):
    step = pl.program_id(0)
    count = interp_ref.shape[0]
    size_x = image.shape[1]

    @pl.when(step == 0)
    def _():
        mix_depth(planes_ref, kh_ref, kl_ref, image, group, size_x)

    def some(part, carry):
        for k in range(unroll):
            local = part * unroll + k
            values = pick_values(
                image, corner_ref, y_ref, row_ref, step * count + local, local, 1
            )
            bend = lax.dot_general(values, interp_ref[local], NT, preferred_element_type=F32)
            out_ref[pl.ds(local, 1), :] = bend[0:1]
        return carry

    lax.fori_loop(0, count // unroll, some, 0)
    prob = prob_ref[...]
    out_ref[...] = prob * (1.0 - prob) * out_ref[...]


def scatter_kernel(slab, unroll, ids_ref, count_ref, z_ref, y_ref, key_ref, term_ref, out_ref):
    cols = y_ref.shape[-1]
    size_y = out_ref.shape[-1]
    rows = BOXZ * slab
    out_ref[...] = jnp.zeros_like(out_ref)

    def some(part, carry):
        sums = []
        for k in range(unroll):
            block = ids_ref[part * unroll + k]
            row_line = lax.broadcasted_iota(jnp.int32, (rows, cols), 0)
            y_line = lax.broadcasted_iota(jnp.int32, (size_y, cols), 0)
            wanted = row_line == key_ref[pl.ds(block, 1), :]
            left = jnp.where(wanted, term_ref[pl.ds(block, 1), :], 0.0).astype(BF16)
            right = jnp.where(y_line == y_ref[pl.ds(block, 1), :], 1.0, 0.0).astype(BF16)
            sums.append((block, lax.dot_general(left, right, NT, preferred_element_type=F32)))
        for block, piece in sums:
            at = pl.multiple_of(z_ref[block] * slab, slab)
            out_ref[pl.ds(at, rows), :] += piece
        return carry

    lax.fori_loop(0, lax.div(count_ref[0] + unroll - 1, unroll), some, 0)


def whole(shape):
    return pl.BlockSpec(
        shape, lambda i, *_: (0,) * len(shape), pipeline_mode=pl.Buffered(buffer_count=1)
    )


def params():
    return pltpu.CompilerParams(
        vmem_limit_bytes=VMEM_BYTES, dimension_semantics=("arbitrary",)
    )


def body(
    grid_weights,
    direction,
    kern_x,
    kern_y,
    kern_z,
    interp,
    block_corner,
    block_offsets,
    labels,
    trial_steps,
    accept,
):
    slab, size_y, size_z = grid_weights.shape
    size_x = kern_x.shape[0]
    devices = lax.axis_size("pts")
    me = lax.axis_index("pts")
    blocks, cols = block_offsets.shape
    per_block = interp.shape[1]
    points = blocks * per_block * devices
    group = max(1, PACK // slab)
    pack = group * slab
    unroll = 4
    count = 16

    spare = jnp.pad(block_corner, ((0, PACK - 3), (0, cols - blocks)))
    sent = jnp.concatenate([block_offsets, spare], axis=0).astype(jnp.int16)
    everyone = lax.all_gather(sent, "pts", axis=0)

    planes = plane_mix(jnp.stack([grid_weights, direction]), kern_y, kern_z)
    planes = planes.reshape(size_z * 2 // group, pack, size_y)
    gathered = lax.all_gather(planes, "pts", axis=0)
    kern_high, kern_low = widen_kern(kern_x, devices, slab, group)

    y_cell = block_corner[1][:, None] + block_offsets // BOXZ % BOXY
    box_row = block_offsets % BOXZ * BOXX + block_offsets // (BOXY * BOXZ)
    chosen = jnp.sum(jnp.where(jnp.arange(NTRIAL) == accept[0], trial_steps, 0.0))

    steps = blocks // count
    rows_of = lambda width: pl.BlockSpec((count, width), lambda i, *_: (i, 0))
    interp_spec = pl.BlockSpec((count, per_block, cols), lambda i, *_: (i, 0, 0))
    pair, probability, column_term, own = pl.pallas_call(
        functools.partial(forward_kernel, group, unroll),
        grid_spec=pltpu.PrefetchScalarGridSpec(
            num_scalar_prefetch=3,
            grid=(steps,),
            in_specs=[
                whole(gathered.shape),
                whole(kern_high.shape),
                whole(kern_low.shape),
                rows_of(cols),
                rows_of(cols),
                rows_of(per_block),
                interp_spec,
            ],
            out_specs=[
                pl.BlockSpec((2, count, per_block), lambda i, *_: (0, i, 0)),
                rows_of(per_block),
                rows_of(cols),
                pl.BlockSpec((2 * size_z, slab, size_y), lambda i, *_: (0, 0, 0)),
            ],
            scratch_shapes=[
                pltpu.VMEM((2 * size_z, size_x, size_y), F32),
                pltpu.VMEM((count, per_block), F32),
            ],
        ),
        out_shape=[
            jax.ShapeDtypeStruct((2, blocks, per_block), F32),
            jax.ShapeDtypeStruct((blocks, per_block), F32),
            jax.ShapeDtypeStruct((blocks, cols), F32),
            jax.ShapeDtypeStruct((2 * size_z, slab, size_y), F32),
        ],
        compiler_params=params(),
        name="forward",
    )(
        block_corner,
        me.astype(jnp.int32).reshape(1),
        chosen.reshape(1),
        gathered,
        kern_high,
        kern_low,
        y_cell,
        box_row,
        labels,
        interp,
    )

    terms = lax.all_gather(column_term.astype(BF16), "pts", axis=0, tiled=True).astype(F32)

    far_offsets = everyone[:, :blocks].astype(jnp.int32).reshape(devices * blocks, cols)
    far = everyone[:, blocks : blocks + 3, :blocks].astype(jnp.int32)
    far_x, far_y, far_z = (far[:, k].reshape(-1) for k in range(3))
    x_from = far_x - me * slab
    far_cell = x_from[:, None] + far_offsets // (BOXY * BOXZ)
    inside = (far_cell >= 0) & (far_cell < slab)
    key = jnp.where(inside, far_offsets % BOXZ * slab + far_cell, -1)
    far_line = far_y[:, None] + far_offsets // BOXZ % BOXY
    total = devices * blocks
    touches = (x_from < slab) & (x_from > -BOXX)
    ranks = jnp.arange(total, dtype=jnp.int32)
    ids = lax.sort(jnp.where(touches, ranks, ranks + total))
    ids = jnp.where(ids >= total, ids - total, ids)
    touched = jnp.sum(touches.astype(jnp.int32)).reshape(1)

    spread = pl.pallas_call(
        functools.partial(scatter_kernel, slab, unroll),
        grid_spec=pltpu.PrefetchScalarGridSpec(
            num_scalar_prefetch=3,
            grid=(1,),
            in_specs=[whole((total, cols))] * 3,
            out_specs=pl.BlockSpec((size_z * slab, size_y), lambda i, *_: (0, 0)),
        ),
        out_shape=jax.ShapeDtypeStruct((size_z * slab, size_y), F32),
        compiler_params=params(),
        name="spread",
    )(ids, touched, far_z, far_line, key, terms)

    new_weights = grid_weights + chosen * direction
    grid_gradient = (
        jnp.transpose(spread.reshape(size_z, slab, size_y), (1, 2, 0)) - new_weights
    )

    fields = own.reshape(size_z, 2, slab, size_y)
    weights_t = jnp.transpose(grid_weights, (2, 0, 1))
    direction_t = jnp.transpose(direction, (2, 0, 1))
    quads = jnp.stack(
        [
            jnp.sum(weights_t * fields[:, 0]),
            jnp.sum(direction_t * fields[:, 0]),
            jnp.sum(direction_t * fields[:, 1]),
        ]
    )
    latent, slope_pt = pair[0], pair[1]
    target = labels.astype(F32)
    signed = 2.0 * target - 1.0
    trial_latent = latent[None] + trial_steps[:, None, None] * slope_pt[None]
    loglik = jnp.sum(jax.nn.log_sigmoid(signed[None] * trial_latent), axis=(1, 2))
    descent = jnp.sum(
        (target[None] - jax.nn.sigmoid(trial_latent)) * slope_pt[None], axis=(1, 2)
    )
    sums = jnp.concatenate([loglik, descent, quads])
    first = high_part(sums)
    second = high_part(sums - first)
    third = sums - first - second
    split = jnp.stack([first, second, third]).astype(BF16)
    split = jnp.pad(split, ((0, pack - 3), (0, size_y - split.shape[1])))

    bend_planes = plane_mix(grid_gradient[None], kern_y, kern_z)
    bend_planes = bend_planes.reshape(size_z // group, pack, size_y)
    bend_sent = jnp.concatenate([bend_planes, split[None], split[None]], axis=0)
    bend_all = lax.all_gather(bend_sent, "pts", axis=0)
    units = size_z // group

    curvature = pl.pallas_call(
        functools.partial(bend_kernel, group, unroll),
        grid_spec=pltpu.PrefetchScalarGridSpec(
            num_scalar_prefetch=1,
            grid=(steps,),
            in_specs=[
                whole((devices, units, pack, size_y)),
                whole(kern_high.shape),
                whole(kern_low.shape),
                rows_of(cols),
                rows_of(cols),
                rows_of(per_block),
                interp_spec,
            ],
            out_specs=rows_of(per_block),
            scratch_shapes=[pltpu.VMEM((size_z, size_x, size_y), F32)],
        ),
        out_shape=jax.ShapeDtypeStruct((blocks, per_block), F32),
        compiler_params=params(),
        name="bend",
    )(
        block_corner,
        bend_all,
        kern_high,
        kern_low,
        y_cell,
        box_row,
        probability,
        interp,
    )

    got = bend_all[:, units, :3, : sums.shape[0]].astype(F32)
    everything = jnp.sum(got, axis=(0, 1))
    loglik = everything[:NTRIAL]
    descent = everything[NTRIAL : 2 * NTRIAL]
    quad_gu, quad_du, quad_dv = (everything[2 * NTRIAL + k] for k in range(3))
    prior = 0.5 * (quad_gu + 2.0 * trial_steps * quad_du + trial_steps * trial_steps * quad_dv)
    trial_objective = (loglik - prior) / points
    trial_slope = (descent - quad_du - trial_steps * quad_dv) / points
    return (new_weights, grid_gradient, curvature, trial_objective, trial_slope)


def solution(mesh):
    return jax.shard_map(
        body,
        mesh=mesh,
        in_specs=(
            P(("parts", "pts"), None, None),
            P(("parts", "pts"), None, None),
            P(),
            P(),
            P(),
            P(("parts", "pts"), None, None),
            P(None, ("parts", "pts")),
            P(("parts", "pts"), None),
            P(("parts", "pts"), None),
            P(),
            P(),
        ),
        out_specs=(
            P(("parts", "pts"), None, None),
            P(("parts", "pts"), None, None),
            P(("parts", "pts"), None),
            P("parts"),
            P("parts"),
        ),
        check_vma=False,
    )
```

```python
import functools

import jax
import jax.numpy as jnp
from jax import lax
from jax.experimental import pallas as pl
from jax.experimental.pallas import tpu as pltpu
from jax.sharding import PartitionSpec as P


BOXX = 16
BOXY = 16
BOXZ = 8
NTRIAL = 5
PACK = 16
VMEM_BYTES = 60 * 1024 * 1024

HIGHEST = lax.Precision.HIGHEST
F32 = jnp.float32
BF16 = jnp.bfloat16
NT = (((1,), (1,)), ((), ()))


def high_part(value):
    return lax.reduce_precision(value, 8, 7)


def plane_mix(fields_zc, kern_y, kern_z):
    inner = jnp.einsum("zc,fabc->zfab", kern_z, fields_zc, precision=HIGHEST)
    return jnp.einsum("zfab,yb->zfay", inner, kern_y, precision=HIGHEST).astype(BF16)


def widen_kern(kern_x, devices, slab, group):
    size_x = kern_x.shape[0]
    parts = kern_x.reshape(1, size_x, devices, 1, slab)
    same = jnp.eye(group, dtype=F32).reshape(group, 1, 1, group, 1)
    wide = (parts * same).reshape(group * size_x, devices * group * slab)
    high = high_part(wide)
    return high.astype(BF16), (wide - high).astype(BF16)


def mix_depth(planes_ref, kh_ref, kl_ref, image, group, size_x):
    devices, units, pack, lanes = planes_ref.shape

    def one(step, carry):
        pair = [
            planes_ref[:, step * 2 + t].reshape(devices * pack, lanes) for t in range(2)
        ]
        rhs = jnp.concatenate(pair, axis=1)
        mixed = jnp.dot(kh_ref[...], rhs, preferred_element_type=F32)
        mixed = mixed + jnp.dot(kl_ref[...], rhs, preferred_element_type=F32)
        for t in range(2):
            for g in range(group):
                image[(step * 2 + t) * group + g] = mixed[
                    g * size_x : (g + 1) * size_x, t * lanes : (t + 1) * lanes
                ]
        return carry

    lax.fori_loop(0, units // 2, one, 0)


def pick_values(image, corner_ref, y_ref, row_ref, block, local, fields):
    size_y = image.shape[-1]
    cols = y_ref.shape[-1]
    box_rows = BOXZ * BOXX
    at_z = corner_ref[2, block]
    at_x = corner_ref[0, block]
    box = image[pl.ds(at_z * fields, BOXZ * fields), pl.ds(at_x, BOXX), :]
    box = box.reshape(fields * box_rows, size_y).astype(BF16)
    y_line = lax.broadcasted_iota(jnp.int32, (size_y, cols), 0)
    pick_y = jnp.where(y_line == y_ref[pl.ds(local, 1), :], 1.0, 0.0).astype(BF16)
    lines = jnp.dot(box, pick_y, preferred_element_type=F32)
    lines = lines.reshape(BOXZ, fields, BOXX, cols)
    row_line = lax.broadcasted_iota(jnp.int32, (box_rows, cols), 0)
    kept = row_line == row_ref[pl.ds(local, 1), :]
    top = lax.broadcasted_iota(jnp.int32, (8, cols), 0)
    stacked = jnp.zeros((8, cols), F32)
    for f in range(fields):
        line = jnp.where(kept, lines[:, f].reshape(box_rows, cols), 0.0)
        value = jnp.sum(line, axis=0, keepdims=True)
        stacked = jnp.where(top == f, value, stacked)
    return stacked.astype(BF16)


def latent_kernel(
    group,
    unroll,
    corner_ref,
    slab_ref,
    planes_ref,
    kh_ref,
    kl_ref,
    y_ref,
    row_ref,
    interp_ref,
    latent_ref,
    own_ref,
    image,
):
    step = pl.program_id(0)
    count = interp_ref.shape[0]
    size_x = image.shape[1]

    @pl.when(step == 0)
    def _():
        mix_depth(planes_ref, kh_ref, kl_ref, image, group, size_x)
        slab = own_ref.shape[1]
        at = pl.multiple_of(slab_ref[0] * slab, slab)
        own_ref[...] = image[:, pl.ds(at, slab), :]

    def some(part, carry):
        for k in range(unroll):
            local = part * unroll + k
            values = pick_values(
                image, corner_ref, y_ref, row_ref, step * count + local, local, 1
            )
            line = lax.dot_general(values, interp_ref[local], NT, preferred_element_type=F32)
            latent_ref[pl.ds(local, 1), :] = line[0:1]
        return carry

    lax.fori_loop(0, count // unroll, some, 0)


def forward_kernel(
    group,
    unroll,
    corner_ref,
    slab_ref,
    chosen_ref,
    planes_ref,
    kh_ref,
    kl_ref,
    y_ref,
    row_ref,
    labels_ref,
    latent_ref,
    interp_ref,
    slope_ref,
    prob_ref,
    col_ref,
    own_ref,
    image,
    res_ref,
    term_ref,
):
    step = pl.program_id(0)
    count = interp_ref.shape[0]
    size_x = image.shape[1]

    @pl.when(step == 0)
    def _():
        mix_depth(planes_ref, kh_ref, kl_ref, image, group, size_x)
        slab = own_ref.shape[1]
        at = pl.multiple_of(slab_ref[0] * slab, slab)
        own_ref[...] = image[:, pl.ds(at, slab), :]

    def some(part, carry):
        for k in range(unroll):
            local = part * unroll + k
            values = pick_values(
                image, corner_ref, y_ref, row_ref, step * count + local, local, 1
            )
            line = lax.dot_general(values, interp_ref[local], NT, preferred_element_type=F32)
            slope_ref[pl.ds(local, 1), :] = line[0:1]
        return carry

    lax.fori_loop(0, count // unroll, some, 0)
    logits = latent_ref[...] + chosen_ref[0] * slope_ref[...]
    prob = jax.nn.sigmoid(logits)
    prob_ref[...] = prob
    res_ref[...] = (labels_ref[...].astype(F32) - prob).astype(BF16).astype(F32)

    def back(part, carry):
        for k in range(unroll):
            local = part * unroll + k
            row = jnp.broadcast_to(res_ref[pl.ds(local, 1), :], (8, res_ref.shape[1]))
            term = jnp.dot(row.astype(BF16), interp_ref[local], preferred_element_type=F32)
            term_ref[pl.ds(local, 1), :] = term[0:1]
        return carry

    lax.fori_loop(0, count // unroll, back, 0)
    col_ref[...] = term_ref[...].astype(BF16)


def bend_kernel(
    group,
    unroll,
    corner_ref,
    planes_ref,
    kh_ref,
    kl_ref,
    y_ref,
    row_ref,
    prob_ref,
    interp_ref,
    out_ref,
    image,
):
    step = pl.program_id(0)
    count = interp_ref.shape[0]
    size_x = image.shape[1]

    @pl.when(step == 0)
    def _():
        mix_depth(planes_ref, kh_ref, kl_ref, image, group, size_x)

    def some(part, carry):
        for k in range(unroll):
            local = part * unroll + k
            values = pick_values(
                image, corner_ref, y_ref, row_ref, step * count + local, local, 1
            )
            bend = lax.dot_general(values, interp_ref[local], NT, preferred_element_type=F32)
            out_ref[pl.ds(local, 1), :] = bend[0:1]
        return carry

    lax.fori_loop(0, count // unroll, some, 0)
    prob = prob_ref[...]
    out_ref[...] = prob * (1.0 - prob) * out_ref[...]


def scatter_kernel(slab, unroll, ids_ref, count_ref, z_ref, y_ref, key_ref, term_ref, out_ref):
    cols = y_ref.shape[-1]
    size_y = out_ref.shape[-1]
    rows = BOXZ * slab
    out_ref[...] = jnp.zeros_like(out_ref)

    def some(part, carry):
        sums = []
        for k in range(unroll):
            block = ids_ref[part * unroll + k]
            row_line = lax.broadcasted_iota(jnp.int32, (rows, cols), 0)
            y_line = lax.broadcasted_iota(jnp.int32, (size_y, cols), 0)
            wanted = row_line == key_ref[pl.ds(block, 1), :]
            left = jnp.where(wanted, term_ref[pl.ds(block, 1), :], 0.0).astype(BF16)
            right = jnp.where(y_line == y_ref[pl.ds(block, 1), :], 1.0, 0.0).astype(BF16)
            sums.append((block, lax.dot_general(left, right, NT, preferred_element_type=F32)))
        for block, piece in sums:
            at = pl.multiple_of(z_ref[block] * slab, slab)
            out_ref[pl.ds(at, rows), :] += piece
        return carry

    lax.fori_loop(0, lax.div(count_ref[0] + unroll - 1, unroll), some, 0)


def whole(shape):
    return pl.BlockSpec(
        shape, lambda i, *_: (0,) * len(shape), pipeline_mode=pl.Buffered(buffer_count=1)
    )


def params():
    return pltpu.CompilerParams(
        vmem_limit_bytes=VMEM_BYTES, dimension_semantics=("arbitrary",)
    )


def body(
    grid_weights,
    direction,
    kern_x,
    kern_y,
    kern_z,
    interp,
    block_corner,
    block_offsets,
    labels,
    trial_steps,
    accept,
):
    slab, size_y, size_z = grid_weights.shape
    size_x = kern_x.shape[0]
    devices = lax.axis_size("pts")
    me = lax.axis_index("pts")
    blocks, cols = block_offsets.shape
    per_block = interp.shape[1]
    points = blocks * per_block * devices
    group = max(1, PACK // slab)
    pack = group * slab
    unroll = 8
    count = 16

    spare = jnp.pad(block_corner, ((0, PACK - 3), (0, cols - blocks)))
    sent = jnp.concatenate([block_offsets, spare], axis=0).astype(jnp.int16)
    units = size_z // group
    sides = []
    for field in (grid_weights, direction):
        planes = plane_mix(field[None], kern_y, kern_z).reshape(units, pack, size_y)
        sides.append(lax.all_gather(planes, "pts", axis=0))
    gathered_w, gathered_d = sides
    gathered_w, sent = lax.optimization_barrier((gathered_w, sent))
    everyone = lax.all_gather(sent, "pts", axis=0)
    kern_high, kern_low = widen_kern(kern_x, devices, slab, group)

    y_cell = block_corner[1][:, None] + block_offsets // BOXZ % BOXY
    box_row = block_offsets % BOXZ * BOXX + block_offsets // (BOXY * BOXZ)
    chosen = jnp.sum(jnp.where(jnp.arange(NTRIAL) == accept[0], trial_steps, 0.0))

    steps = blocks // count
    rows_of = lambda width: pl.BlockSpec((count, width), lambda i, *_: (i, 0))
    interp_spec = pl.BlockSpec((count, per_block, cols), lambda i, *_: (i, 0, 0))
    work = pl.CostEstimate(
        flops=4 * blocks * size_y * size_y * cols,
        bytes_accessed=gathered_w.size * 2 + interp.size * 2,
        transcendentals=0,
    )
    mine = me.astype(jnp.int32).reshape(1)
    own_spec = pl.BlockSpec((size_z, slab, size_y), lambda i, *_: (0, 0, 0))
    own_shape = jax.ShapeDtypeStruct((size_z, slab, size_y), F32)
    point_shape = jax.ShapeDtypeStruct((blocks, per_block), F32)
    image_scratch = pltpu.VMEM((size_z, size_x, size_y), F32)
    latent, own_w = pl.pallas_call(
        functools.partial(latent_kernel, group, unroll),
        grid_spec=pltpu.PrefetchScalarGridSpec(
            num_scalar_prefetch=2,
            grid=(steps,),
            in_specs=[
                whole(gathered_w.shape),
                whole(kern_high.shape),
                whole(kern_low.shape),
                rows_of(cols),
                rows_of(cols),
                interp_spec,
            ],
            out_specs=[rows_of(per_block), own_spec],
            scratch_shapes=[image_scratch],
        ),
        out_shape=[point_shape, own_shape],
        compiler_params=params(),
        cost_estimate=work,
        name="latent",
    )(block_corner, mine, gathered_w, kern_high, kern_low, y_cell, box_row, interp)

    forward = pl.pallas_call(
        functools.partial(forward_kernel, group, unroll),
        grid_spec=pltpu.PrefetchScalarGridSpec(
            num_scalar_prefetch=3,
            grid=(steps,),
            in_specs=[
                whole(gathered_d.shape),
                whole(kern_high.shape),
                whole(kern_low.shape),
                rows_of(cols),
                rows_of(cols),
                rows_of(per_block),
                rows_of(per_block),
                interp_spec,
            ],
            out_specs=[
                rows_of(per_block),
                rows_of(per_block),
                rows_of(cols),
                own_spec,
            ],
            scratch_shapes=[image_scratch, pltpu.VMEM((count, per_block), F32), pltpu.VMEM((count, cols), F32)],
        ),
        out_shape=[
            point_shape,
            point_shape,
            jax.ShapeDtypeStruct((blocks, cols), BF16),
            own_shape,
        ],
        compiler_params=params(),
        cost_estimate=work,
        name="forward",
    )
    slope_pt, probability, column_term, own_d = forward(
        block_corner,
        mine,
        chosen.reshape(1),
        gathered_d,
        kern_high,
        kern_low,
        y_cell,
        box_row,
        labels,
        latent,
        interp,
    )

    terms = lax.all_gather(column_term, "pts", axis=0, tiled=True).astype(F32)

    far_offsets = everyone[:, :blocks].astype(jnp.int32).reshape(devices * blocks, cols)
    far = everyone[:, blocks : blocks + 3, :blocks].astype(jnp.int32)
    far_x, far_y, far_z = (far[:, k].reshape(-1) for k in range(3))
    x_from = far_x - me * slab
    far_cell = x_from[:, None] + far_offsets // (BOXY * BOXZ)
    inside = (far_cell >= 0) & (far_cell < slab)
    key = jnp.where(inside, far_offsets % BOXZ * slab + far_cell, -1)
    far_line = far_y[:, None] + far_offsets // BOXZ % BOXY
    total = devices * blocks
    touches = (x_from < slab) & (x_from > -BOXX)
    ranks = jnp.arange(total, dtype=jnp.int32)
    ids = lax.sort(jnp.where(touches, ranks, ranks + total))
    ids = jnp.where(ids >= total, ids - total, ids)
    touched = jnp.sum(touches.astype(jnp.int32)).reshape(1)

    spread = pl.pallas_call(
        functools.partial(scatter_kernel, slab, unroll),
        grid_spec=pltpu.PrefetchScalarGridSpec(
            num_scalar_prefetch=3,
            grid=(1,),
            in_specs=[whole((total, cols))] * 3,
            out_specs=pl.BlockSpec((size_z * slab, size_y), lambda i, *_: (0, 0)),
        ),
        out_shape=jax.ShapeDtypeStruct((size_z * slab, size_y), F32),
        compiler_params=params(),
        name="spread",
    )(ids, touched, far_z, far_line, key, terms)

    new_weights = grid_weights + chosen * direction
    grid_gradient = (
        jnp.transpose(spread.reshape(size_z, slab, size_y), (1, 2, 0)) - new_weights
    )

    weights_t = jnp.transpose(grid_weights, (2, 0, 1))
    direction_t = jnp.transpose(direction, (2, 0, 1))
    quads = jnp.stack(
        [
            jnp.sum(weights_t * own_w),
            jnp.sum(direction_t * own_w),
            jnp.sum(direction_t * own_d),
        ]
    )
    target = labels.astype(F32)
    signed = 2.0 * target - 1.0
    trial_latent = latent[None] + trial_steps[:, None, None] * slope_pt[None]
    loglik = jnp.sum(jax.nn.log_sigmoid(signed[None] * trial_latent), axis=(1, 2))
    descent = jnp.sum(
        (target[None] - jax.nn.sigmoid(trial_latent)) * slope_pt[None], axis=(1, 2)
    )
    sums = jnp.concatenate([loglik, descent, quads])
    first = high_part(sums)
    second = high_part(sums - first)
    third = sums - first - second
    split = jnp.stack([first, second, third]).astype(BF16)
    split = jnp.pad(split, ((0, pack - 3), (0, size_y - split.shape[1])))

    bend_planes = plane_mix(grid_gradient[None], kern_y, kern_z)
    bend_planes = bend_planes.reshape(size_z // group, pack, size_y)
    bend_sent = jnp.concatenate([bend_planes, split[None], split[None]], axis=0)
    bend_all = lax.all_gather(bend_sent, "pts", axis=0)
    curvature = pl.pallas_call(
        functools.partial(bend_kernel, group, unroll),
        grid_spec=pltpu.PrefetchScalarGridSpec(
            num_scalar_prefetch=1,
            grid=(steps,),
            in_specs=[
                whole((devices, units, pack, size_y)),
                whole(kern_high.shape),
                whole(kern_low.shape),
                rows_of(cols),
                rows_of(cols),
                rows_of(per_block),
                interp_spec,
            ],
            out_specs=rows_of(per_block),
            scratch_shapes=[pltpu.VMEM((size_z, size_x, size_y), F32)],
        ),
        out_shape=jax.ShapeDtypeStruct((blocks, per_block), F32),
        compiler_params=params(),
        name="bend",
    )(
        block_corner,
        bend_all,
        kern_high,
        kern_low,
        y_cell,
        box_row,
        probability,
        interp,
    )

    got = bend_all[:, units, :3, : sums.shape[0]].astype(F32)
    everything = jnp.sum(got, axis=(0, 1))
    loglik = everything[:NTRIAL]
    descent = everything[NTRIAL : 2 * NTRIAL]
    quad_gu, quad_du, quad_dv = (everything[2 * NTRIAL + k] for k in range(3))
    prior = 0.5 * (quad_gu + 2.0 * trial_steps * quad_du + trial_steps * trial_steps * quad_dv)
    trial_objective = (loglik - prior) / points
    trial_slope = (descent - quad_du - trial_steps * quad_dv) / points
    return (new_weights, grid_gradient, curvature, trial_objective, trial_slope)


def solution(mesh):
    return jax.shard_map(
        body,
        mesh=mesh,
        in_specs=(
            P(("parts", "pts"), None, None),
            P(("parts", "pts"), None, None),
            P(),
            P(),
            P(),
            P(("parts", "pts"), None, None),
            P(None, ("parts", "pts")),
            P(("parts", "pts"), None),
            P(("parts", "pts"), None),
            P(),
            P(),
        ),
        out_specs=(
            P(("parts", "pts"), None, None),
            P(("parts", "pts"), None, None),
            P(("parts", "pts"), None),
            P("parts"),
            P("parts"),
        ),
        check_vma=False,
    )
```
